32 devices in a mesh: groups: 2 (over y), seq: 4 (over z), adapter: 2 (over x), head: 2 (over core).
Axes of the slice: x: 2, y: 2, z: 4, core: 2. Of those that a mesh axis runs over, the one named last changes fastest.
Arguments:
- hidden: bfloat16 [64, 3, 8192], P(('groups', 'seq', 'adapter'), None, 'head'), parts along dimension 0, may hold values from -6 to 6
- base_query_rows: bfloat16 [64, 3, 8192], P(('groups', 'seq', 'adapter'), None, 'head'), parts along dimension 0, may hold values from -16 to 16
- fresh_key_value: bfloat16 [2, 64, 3, 1024], P(None, ('groups', 'seq', 'adapter'), None, 'head'), parts along dimension 1, may hold values from -12 to 12
- suffix_key_value: bfloat16 [2, 64, 32, 1024], P(None, ('groups', 'seq', 'adapter'), None, 'head'), parts along dimension 1, may hold values from -12 to 12
- suffix_length: int32 [64], P(('groups', 'seq', 'adapter')), parts along dimension 0, may hold values from 0 to 32, as said below
- row_adapter_index: int32 [64, 1], P(('groups', 'seq', 'adapter')), parts along dimension 0, may hold values from 0 to 1
- prompt_key_value: bfloat16 [2, 8192, 1024], P(None, ('groups', 'seq'), 'head'), parts along dimension 1, may hold values from -16 to 16
- query_down_factors: bfloat16 [4, 64, 8192], P(('groups', 'adapter'), None, 'head'), parts along dimension 0, may hold values from -0.0625 to 0.0625
- query_up_factors: bfloat16 [4, 64, 8192], P(('groups', 'adapter'), None, 'head'), parts along dimension 0, may hold values from -0.75 to 0.75
- output_down_factors: bfloat16 [4, 64, 8192], P(('groups', 'adapter'), None, 'head'), parts along dimension 0, may hold values from -0.0625 to 0.0625
- output_up_factors: bfloat16 [4, 64, 8192], P(('groups', 'adapter'), None, 'head'), parts along dimension 0, may hold values from -0.75 to 0.75
Outputs:
- attended: bfloat16 [64, 3, 8192], P(('groups', 'seq', 'adapter'), None, 'head'), parts along dimension 0
- adapted: bfloat16 [64, 3, 8192], P(('groups', 'seq', 'adapter'), None, 'head'), parts along dimension 0
The draws below stay inside these ranges and needn't reach their ends.
There are 2 independent parts, one for each index of `groups`. The reference program is written for one: setup_inputs(seed, part) draws one part's arguments, and reference() takes and returns one part's arrays. A program takes and returns all parts, laid end to end along the dimension named above; each array names one. Nothing has to cross between parts.
Inputs may be any that keep to these rules, and one draw needn't show every extreme that they name: `suffix_length`: each row's suffix holds at most 32 tokens, and some row holds exactly 32.
All inputs are finite; a program needn't handle non-finite values.
Results may differ from the reference program's by a relative error of at most 0.011.
Values may be sent and summed in bfloat16 or wider, within the bound.
A program may use at most 64 MiB of HBM per device.

```python
import math
import jax
import jax.numpy as jnp
from jax import lax

MODEL_WIDTH = 8192
QUERY_HEADS = 64
KVH = 8
HEAD_SIZE = 128
FACTOR_RANK = 64
STEPS = 3
P_DEV = 1024
SUF = 32
ADAPTER_TOTAL = 2
ROWS = 32
PROMPT = 4096
N_SEQ = 4


def draw_base_query_rows(key, part):
    values = jax.random.truncated_normal(key, -6.0, 6.0, (ROWS, STEPS, QUERY_HEADS, HEAD_SIZE), jnp.float32)
    return values.reshape(ROWS, STEPS, QUERY_HEADS * HEAD_SIZE).astype(jnp.bfloat16)


def draw_prompt_key_value(key, part):
    first_key, second_key = jax.random.split(jax.random.fold_in(key, 17))
    keys_part = 2.0 * jax.random.truncated_normal(first_key, -8.0, 8.0, (PROMPT, KVH, HEAD_SIZE), jnp.float32)
    values_part = jax.random.truncated_normal(second_key, -6.0, 6.0, (PROMPT, KVH * HEAD_SIZE), jnp.float32)
    return jnp.stack([keys_part.reshape(PROMPT, KVH * HEAD_SIZE), values_part]).astype(jnp.bfloat16)


def draw_suffix_length(key, part):
    lengths = jax.random.randint(jax.random.fold_in(key, 29), (ROWS,), 0, SUF + 1)
    return lengths.at[0].set(SUF)


def block_scale(rng, extent, cuts, smallest, high):
    factor_of = 1.0
    for axis_at, blocks in cuts:
        heights = jax.random.uniform(jax.random.fold_in(jax.random.fold_in(rng, 6), axis_at), (blocks,), jnp.float32, smallest / len(cuts), high / len(cuts))
        factor_of = factor_of * jnp.repeat(jnp.exp(heights), extent[axis_at] // blocks).reshape((-1,) + (1,) * (len(extent) - 1 - axis_at))
    return factor_of


def choose_distinct(stream_key, rows, amount, top, lift):
    sequence = jax.random.permutation(jax.random.fold_in(stream_key, 1), amount)
    favour = sequence
    for power in range(3):
        favour = favour * favour // amount
    favour = favour * lift // amount
    tickets = jax.random.randint(jax.random.fold_in(stream_key, 2), (rows, amount), 0, 4096) + favour
    fixed_rows = jax.random.permutation(jax.random.fold_in(stream_key, 3), rows)[jnp.arange(amount) % rows]
    tickets = jnp.where(jnp.arange(rows)[:, None] == fixed_rows[None, :], 1 << 14, tickets)
    priority = tickets * amount + jnp.arange(amount)
    return lax.top_k(priority.astype(jnp.int32), top)[1].astype(jnp.int32)


def gaussian(key, shape, width, most, cuts=(), kind=jnp.bfloat16):
    values = jax.random.normal(key, shape, jnp.float32) * width
    if len(cuts) > 0:
        values = block_scale(key, shape, cuts, -0.22, 0.18) * values
    return jnp.clip(values, min=-most, max=most).astype(kind)


def setup_inputs(seed: int = 0, part: int = 0) -> dict:
    streams_of = jax.random.split(jax.random.key(seed), 12)
    part_splits = jax.random.split(jax.random.fold_in(streams_of[11], part), 12)
    hidden = gaussian(part_splits[0], (ROWS, STEPS, MODEL_WIDTH), 1.0, 6.0, ((0, 8), (2, 2)))
    base_query_rows = draw_base_query_rows(jax.random.fold_in(jax.random.fold_in(streams_of[11], part), 71), part)
    fresh_key_value = gaussian(part_splits[2], (2, ROWS, STEPS, KVH * HEAD_SIZE), 2.0, 12.0, ((1, 8), (3, 2)))
    suffix_key_value = gaussian(part_splits[3], (2, ROWS, SUF, KVH * HEAD_SIZE), 2.0, 12.0, ((1, 8), (3, 2)))
    suffix_length = draw_suffix_length(jax.random.fold_in(jax.random.fold_in(streams_of[11], part), 71), part)
    row_adapter_index = choose_distinct(part_splits[5], ROWS, ADAPTER_TOTAL, 1, 4096)
    prompt_key_value = draw_prompt_key_value(jax.random.fold_in(jax.random.fold_in(streams_of[11], part), 71), part)
    query_down_factors = gaussian(part_splits[7], (ADAPTER_TOTAL, FACTOR_RANK, MODEL_WIDTH), MODEL_WIDTH ** -0.5, 0.0625, ((0, 2), (2, 2)))
    query_up_factors = gaussian(part_splits[8], (ADAPTER_TOTAL, FACTOR_RANK, QUERY_HEADS * HEAD_SIZE), FACTOR_RANK ** -0.5, 0.75, ((0, 2), (2, 2)))
    output_down_factors = gaussian(part_splits[9], (ADAPTER_TOTAL, FACTOR_RANK, QUERY_HEADS * HEAD_SIZE), (QUERY_HEADS * HEAD_SIZE) ** -0.5, 0.0625, ((0, 2), (2, 2)))
    output_up_factors = gaussian(part_splits[10], (ADAPTER_TOTAL, FACTOR_RANK, MODEL_WIDTH), FACTOR_RANK ** -0.5, 0.75, ((0, 2), (2, 2)))
    return dict(hidden=hidden, base_query_rows=base_query_rows, fresh_key_value=fresh_key_value, suffix_key_value=suffix_key_value, suffix_length=suffix_length, row_adapter_index=row_adapter_index, prompt_key_value=prompt_key_value, query_down_factors=query_down_factors, query_up_factors=query_up_factors, output_down_factors=output_down_factors, output_up_factors=output_up_factors)


rope_base = 1000000.0

def rotate(values_in, position):
    half_dim = values_in.shape[-1] // 2
    frequency = rope_base ** (-2.0 * jnp.arange(half_dim, dtype=jnp.float32) / values_in.shape[-1])
    angles = position[..., None] * frequency
    cos_part = jnp.cos(angles)
    sin_part = jnp.sin(angles)
    first_half = values_in[..., :half_dim]
    second_half = values_in[..., half_dim:]
    return jnp.concatenate([first_half * cos_part - second_half * sin_part, second_half * cos_part + first_half * sin_part], -1)

def rounded_values(values_in):
    narrow = lax.optimization_barrier(values_in.astype(jnp.bfloat16))
    return narrow.astype(jnp.float32)

def down_projected(inputs, factors, adapter_of_row):

    def add_adapter(carried, pair):
        factor, index = pair
        term = jnp.einsum('rsc,kc->rsk', inputs, factor.astype(jnp.float32))
        picked = (adapter_of_row == index)[:, None, None]
        return (carried + jnp.where(picked, term, 0.0), None)
    start = jnp.zeros(inputs.shape[:2] + (factors.shape[1],), jnp.float32)
    result, unused = lax.scan(add_adapter, start, (factors, jnp.arange(factors.shape[0], dtype=jnp.int32)))
    return result

def up_projected(inputs, factors, adapter_of_row):

    def add_adapter(carried, pair):
        factor, index = pair
        term = jnp.einsum('rsk,kc->rsc', inputs, factor.astype(jnp.float32))
        picked = (adapter_of_row == index)[:, None, None]
        return (carried + jnp.where(picked, term, 0.0), None)
    start = jnp.zeros(inputs.shape[:2] + (factors.shape[2],), jnp.float32)
    result, unused = lax.scan(add_adapter, start, (factors, jnp.arange(factors.shape[0], dtype=jnp.int32)))
    return result

def combine_parts(former, latter):
    weighted_a, peaks_a, totals_a = former
    weighted_b, peaks_b, totals_b = latter
    peaks = jnp.maximum(peaks_a, peaks_b)
    factor_a = jnp.exp(peaks_a - peaks)
    factor_b = jnp.exp(peaks_b - peaks)
    return (weighted_a * factor_a[..., None] + weighted_b * factor_b[..., None], peaks, totals_a * factor_a + totals_b * factor_b)

def reference(hidden, base_query_rows, fresh_key_value, suffix_key_value, suffix_length, row_adapter_index, prompt_key_value, query_down_factors, query_up_factors, output_down_factors, output_up_factors):
    adapter_of_row = row_adapter_index[:, 0]
    group_size = QUERY_HEADS // KVH
    score_scale = 1.0 / math.sqrt(HEAD_SIZE)
    query_low_rank = rounded_values(down_projected(hidden.astype(jnp.float32), query_down_factors, adapter_of_row))
    query_adjustment = up_projected(query_low_rank, query_up_factors, adapter_of_row)
    position = (PROMPT + suffix_length[:, None] + jnp.arange(STEPS, dtype=jnp.int32)[None, :]).astype(jnp.float32)
    merged = (base_query_rows.astype(jnp.float32) + query_adjustment).reshape(ROWS, STEPS, QUERY_HEADS, HEAD_SIZE)
    grouped = rounded_values(rotate(merged, position[:, :, None])).reshape(ROWS, STEPS, KVH, group_size, HEAD_SIZE)
    local_keys = jnp.concatenate([suffix_key_value[0], fresh_key_value[0]], 1).astype(jnp.float32).reshape(ROWS, SUF + STEPS, KVH, HEAD_SIZE)
    local_values = jnp.concatenate([suffix_key_value[1], fresh_key_value[1]], 1).astype(jnp.float32).reshape(ROWS, SUF + STEPS, KVH, HEAD_SIZE)
    scores = jnp.einsum('rtkgd,rpkd->rtkgp', grouped, local_keys) * score_scale
    key_slot = jnp.arange(SUF + STEPS, dtype=jnp.int32)[None, None, :]
    admitted = jnp.where(key_slot < SUF, key_slot < suffix_length[:, None, None], key_slot - SUF <= jnp.arange(STEPS, dtype=jnp.int32)[None, :, None])
    admitted = admitted[:, :, None, None, :]
    masked = jnp.where(admitted, scores, -1e+30)
    local_peaks = lax.optimization_barrier(jnp.max(masked, -1))
    local_weight = rounded_values(jnp.where(admitted, jnp.exp(masked - local_peaks[..., None]), 0.0))
    local_weighted = jnp.einsum('rtkgp,rpkd->rtkgd', local_weight, local_values)
    local_totals = lax.optimization_barrier(jnp.sum(local_weight, -1))
    token_count = ROWS * STEPS
    local_part = (local_weighted.reshape(token_count, KVH, group_size, HEAD_SIZE), local_peaks.reshape(token_count, KVH, group_size), local_totals.reshape(token_count, KVH, group_size))
    flat_query = grouped.reshape(token_count, KVH, group_size, HEAD_SIZE)
    prompt_keys = prompt_key_value[0].reshape(N_SEQ, P_DEV, KVH, HEAD_SIZE)
    prompt_values = prompt_key_value[1].reshape(N_SEQ, P_DEV, KVH, HEAD_SIZE)

    def add_block(carried, pair):
        block_keys, block_values = pair
        block_scores = jnp.einsum('nkgd,pkd->nkgp', flat_query, block_keys.astype(jnp.float32)) * score_scale
        peaks = lax.optimization_barrier(jnp.max(block_scores, -1))
        weight = rounded_values(jnp.exp(block_scores - peaks[..., None]))
        weighted = jnp.einsum('nkgp,pkd->nkgd', weight, block_values.astype(jnp.float32))
        totals = lax.optimization_barrier(jnp.sum(weight, -1))
        return (combine_parts(carried, (weighted, peaks, totals)), None)
    combined, unused = lax.scan(add_block, local_part, (prompt_keys, prompt_values))
    attended = (combined[0] / combined[2][..., None]).reshape(ROWS, STEPS, QUERY_HEADS * HEAD_SIZE).astype(jnp.bfloat16)
    attended_full_width = lax.optimization_barrier(attended).astype(jnp.float32)
    output_rank_rows = rounded_values(down_projected(attended_full_width, output_down_factors, adapter_of_row))
    adapted = up_projected(output_rank_rows, output_up_factors, adapter_of_row).astype(jnp.bfloat16)
    return (attended, adapted)
```

```python
import functools
import math

import jax
import jax.numpy as jnp
import numpy as np
from jax import lax
from jax.experimental import pallas as pl
from jax.experimental.pallas import tpu as pltpu
from jax.sharding import PartitionSpec as P

HEAD_SIZE = 128
ROPE_BASE = 1000000.0
MESH = pl.DeviceIdType.MESH
NT = (((1,), (1,)), ((), ()))


def dot_nt(a, b):
    return lax.dot_general(a, b, NT, preferred_element_type=jnp.float32)


def dot_nn(a, b):
    return jnp.dot(a, b, preferred_element_type=jnp.float32)


def body(
    cfg,
    len_ref,
    id_ref,
    cos_ref,
    sin_ref,
    hidden_hbm,
    base_hbm,
    fresh_hbm,
    suffix_hbm,
    prompt_hbm,
    qd_hbm,
    qu_hbm,
    od_hbm,
    ou_hbm,
    att_ref,
    ada_ref,
    hidden_v,
    base_v,
    fresh_v,
    suffix_v,
    prompt_v,
    qd_v,
    qu_v,
    od_v,
    ou_v,
    local_sem,
    hid_in,
    tok_f32,
    rows_f32,
    fresh_pad,
    fresh_f32,
    rk_out,
    rk_in,
    ork_out,
    ork_in,
    dl_out,
    dl_in,
    q_own,
    q_in,
    part_out,
    part_in,
    stat_out,
    stat_in,
    own_o,
    own_m,
    own_t,
    at_out,
    at_in,
    ad_out,
    ad_in,
    hid_s,
    hid_r,
    rk_s,
    rk_r,
    ork_s,
    ork_r,
    dl_s,
    dl_r,
    q_s,
    q_r,
    part_s,
    part_r,
    stat_s,
    stat_r,
    at_s,
    at_r,
    ad_s,
    ad_r,
):
    NS, NA, NH, R, T, KV, G, S = cfg
    D = HEAD_SIZE
    N = R * T
    NG = N * G
    C = G * D
    seq, ada, head = lax.axis_index("seq"), lax.axis_index("adapter"), lax.axis_index("head")
    scale = math.log2(math.e) / math.sqrt(D)

    def at_axis(axis, me, offset, size):
        return {axis: lax.rem(me + offset, size)}

    partners = (
        [at_axis("adapter", ada, d, NA) for d in range(1, NA)]
        + [at_axis("head", head, d, NH) for d in range(1, NH)]
        + [at_axis("seq", seq, d, NS) for d in range(1, NS)]
    )
    barrier = pltpu.get_barrier_semaphore()
    for partner in partners:
        pl.semaphore_signal(barrier, inc=1, device_id=partner, device_id_type=MESH)

    loads = []
    for i, (src, dst) in enumerate(
        (
            (hidden_hbm, hidden_v),
            (qd_hbm, qd_v),
            (qu_hbm, qu_v),
            (base_hbm, base_v),
            (prompt_hbm, prompt_v),
            (suffix_hbm, suffix_v),
            (fresh_hbm, fresh_v),
            (od_hbm, od_v),
            (ou_hbm, ou_v),
        )
    ):
        load = pltpu.make_async_copy(src, dst, local_sem.at[i])
        load.start()
        loads.append(load)
    l_hid, l_qd, l_qu, l_base, l_prompt, l_suffix, l_fresh, l_od, l_ou = loads

    pl.semaphore_wait(barrier, len(partners))

    sends = []

    def send(src, dst, s_sem, r_sem, device):
        copy = pltpu.make_async_remote_copy(
            src_ref=src,
            dst_ref=dst,
            send_sem=s_sem,
            recv_sem=r_sem,
            device_id=device,
            device_id_type=MESH,
        )
        copy.start()
        sends.append(copy)
        return copy

    hid = {}
    for d in range(1, NA):
        hid[d] = send(
            hidden_hbm, hid_in.at[d - 1], hid_s.at[d - 1], hid_r.at[d - 1],
            at_axis("adapter", ada, d, NA),
        )

    def gather_tokens(ref):
        for r in range(R):
            tok_f32[r * T : (r + 1) * T, :] = ref[r].astype(jnp.float32)
        return tok_f32[...].astype(jnp.bfloat16)

    rk = {}

    def rank_part(tokens, factors, slot, out_ref, in_ref, s_sem, r_sem):
        out_ref[slot] = dot_nt(tokens, factors)
        send_rank(slot, out_ref, in_ref, s_sem, r_sem)

    def send_rank(slot, out_ref, in_ref, s_sem, r_sem):
        for j in range(1, NH):
            rk[(slot, j)] = send(
                out_ref.at[slot], in_ref.at[j - 1, slot], s_sem.at[j - 1, slot],
                r_sem.at[j - 1, slot], at_axis("head", head, j, NH),
            )

    def rank_whole(slot, out_ref, in_ref):
        total = out_ref[slot]
        for j in range(1, NH):
            rk[(slot, j)].wait_recv()
            total = total + in_ref[j - 1, slot]
        return total.astype(jnp.bfloat16)

    l_hid.wait()
    l_qd.wait()
    rank_part(gather_tokens(hidden_v), qd_v[0], 0, rk_out, rk_in, rk_s, rk_r)
    for d in range(1, NA):
        hid[d].wait_recv()
        rank_part(gather_tokens(hid_in.at[d - 1]), qd_v[0], d, rk_out, rk_in, rk_s, rk_r)

    def to_rows(x):
        for g in range(G):
            rows_f32[pl.ds(g, N, stride=G), :] = x[:, g * D : (g + 1) * D]
        return rows_f32[...]

    def from_rows(x):
        rows_f32[...] = x
        return jnp.concatenate([rows_f32[pl.ds(g, N, stride=G), :] for g in range(G)], 1)

    def put_out(ref, x, k):
        rows_f32[...] = x
        for r in range(R):
            ref[r, :, k * C : (k + 1) * C] = jnp.concatenate(
                [rows_f32[pl.ds(r * T * G + g, T, stride=G), :] for g in range(G)], 1
            ).astype(jnp.bfloat16)

    l_fresh.wait()
    fresh_pad[...] = jnp.zeros_like(fresh_pad)
    for i in range(2):
        fresh_f32[...] = jnp.zeros_like(fresh_f32)
        for r in range(R):
            fresh_f32[r * T : (r + 1) * T, :] = fresh_v[i, r].astype(jnp.float32)
        fresh_pad[i, 0 : fresh_f32.shape[0], :] = fresh_f32[...].astype(jnp.bfloat16)

    l_qu.wait()
    dl = {}
    for d in range(1, NA):
        rank = rank_whole(d, rk_out, rk_in)
        for k in range(KV):
            dl_out[d - 1, k] = to_rows(
                dot_nn(rank, qu_v[0, :, k * C : (k + 1) * C])
            ).astype(jnp.bfloat16)
            dl[(d, k)] = send(
                dl_out.at[d - 1, k], dl_in.at[d - 1, k], dl_s.at[d - 1, k],
                dl_r.at[d - 1, k], at_axis("adapter", ada, NA - d, NA),
            )
    row_of = lax.broadcasted_iota(jnp.int32, (NG, D), 0)
    lane = lax.broadcasted_iota(jnp.int32, (NG, D), 1)
    eye = row_of == lane
    row_index = row_of // (T * G)
    ids = jnp.zeros((NG, D), jnp.int32)
    lengths = jnp.zeros((NG, D), jnp.int32)
    for r in range(R):
        ids = jnp.where(row_index == r, id_ref[r, 0], ids)
        lengths = jnp.where(row_index == r, len_ref[r], lengths)
    step_of = (row_of - row_index * (T * G)) // G

    def pick(own, ref, k):
        out = own
        for d in range(1, NA):
            out = jnp.where(
                ids == lax.rem(ada + d, NA), ref[d - 1, k].astype(jnp.float32), out
            )
        return out

    cos = jnp.concatenate(
        [jnp.broadcast_to(cos_ref[pl.ds(len_ref[n // T] + n % T, 1), :], (G, D)) for n in range(N)], 0
    )
    sin = jnp.concatenate(
        [jnp.broadcast_to(sin_ref[pl.ds(len_ref[n // T] + n % T, 1), :], (G, D)) for n in range(N)], 0
    )

    rank = rank_whole(0, rk_out, rk_in)
    l_base.wait()
    qs = {}
    order = sorted(range(1, NS), key=lambda d: (min(d, NS - d), d))
    for k in range(KV):
        delta = to_rows(dot_nn(rank, qu_v[0, :, k * C : (k + 1) * C]))
        for r in range(R):
            x = base_v[r, :, k * C : (k + 1) * C].astype(jnp.float32)
            for g in range(G):
                rows_f32[pl.ds(r * T * G + g, T, stride=G), :] = x[:, g * D : (g + 1) * D]
        base = rows_f32[...]
        for d in range(1, NA):
            dl[(d, k)].wait_recv()
        merged = base + pick(delta, dl_in, k)
        turned = merged * cos + pltpu.roll(merged, D // 2, 1) * sin
        q_own[k] = turned.astype(jnp.bfloat16)
        for d in order:
            qs[(d, k)] = send(
                q_own.at[k], q_in.at[d - 1, k], q_s.at[d - 1, k], q_r.at[d - 1, k],
                at_axis("seq", seq, d, NS),
            )

    l_prompt.wait()
    l_suffix.wait()

    def values_of(v):
        return jnp.concatenate([v, jnp.ones((v.shape[0], D), jnp.bfloat16)], 1)

    def prompt_part(query, k):
        cols = slice(k * D, (k + 1) * D)
        scores = dot_nt(query, prompt_v[0, :, cols])
        peak = jnp.max(scores, -1, keepdims=True)
        weight = jnp.exp2((scores - peak) * scale).astype(jnp.bfloat16)
        both = dot_nn(weight, values_of(prompt_v[1, :, cols]))
        return both[:, :D], peak, both[:, D:]

    def local_part(query, k):
        cols = slice(k * D, (k + 1) * D)
        n_suf = R * S
        s_keys = suffix_v[0, :, :, cols].reshape(n_suf, D)
        s_vals = suffix_v[1, :, :, cols].reshape(n_suf, D)
        scores = jnp.concatenate(
            [dot_nt(query, s_keys), dot_nt(query, fresh_pad[0, :, cols])], 1
        )
        masked = jnp.where(admitted, scores, -1e30)
        peak = jnp.max(masked, -1, keepdims=True)
        weight = jnp.where(admitted, jnp.exp2((masked - peak) * scale), 0.0).astype(jnp.bfloat16)
        both = dot_nn(
            weight, values_of(jnp.concatenate([s_vals, fresh_pad[1, :, cols]], 0))
        )
        return both[:, :D], peak, both[:, D:]

    n_suf = R * S
    s_row = lax.broadcasted_iota(jnp.int32, (NG, n_suf), 0) // (T * G)
    s_col = lax.broadcasted_iota(jnp.int32, (NG, n_suf), 1)
    s_len = jnp.concatenate([lengths] * (n_suf // D), 1)
    in_suffix = (s_col // S == s_row) & (s_col - s_row * S < s_len)
    f_slot = lane - row_index * T
    in_fresh = (f_slot >= 0) & (f_slot <= step_of)
    admitted = jnp.concatenate(
        [in_suffix.astype(jnp.int32), in_fresh.astype(jnp.int32)], 1
    ) != 0

    def merge(parts):
        top = functools.reduce(jnp.maximum, [p[1] for p in parts])
        factors = [jnp.exp2((p[1] - top) * scale) for p in parts]
        num = functools.reduce(jnp.add, [p[0] * f for p, f in zip(parts, factors)])
        den = functools.reduce(jnp.add, [p[2] * f for p, f in zip(parts, factors)])
        return num, top, den

    for k in range(KV):
        query = q_own[k]
        o, m, t = merge([prompt_part(query, k), local_part(query, k)])
        own_o[k] = o
        own_m[k] = jnp.broadcast_to(m, (NG, D))
        own_t[k] = t

    parts, stats = {}, {}

    def remote_parts(k):
        for d in order:
            qs[(d, k)].wait_recv()
            o, m, t = prompt_part(q_in[d - 1, k], k)
            part_out[d - 1, k] = o.astype(jnp.bfloat16)
            stat_out[d - 1, k, 0:1, 0:D] = jnp.sum(jnp.where(eye, m, 0.0), 0, keepdims=True)
            stat_out[d - 1, k, 1:2, 0:D] = jnp.sum(jnp.where(eye, t, 0.0), 0, keepdims=True)
            home = at_axis("seq", seq, NS - d, NS)
            parts[(d, k)] = send(
                part_out.at[d - 1, k], part_in.at[d - 1, k], part_s.at[d - 1, k],
                part_r.at[d - 1, k], home,
            )
            stats[(d, k)] = send(
                stat_out.at[d - 1, k], stat_in.at[d - 1, k], stat_s.at[d - 1, k],
                stat_r.at[d - 1, k], home,
            )

    at = {}
    own_rank = [jnp.zeros((N, od_v.shape[1]), jnp.float32)]

    def column(row):
        return jnp.sum(jnp.where(eye, row, 0.0), 1, keepdims=True)

    def combine(k):
        pieces = [(own_o[k], own_m[k], own_t[k])]
        for d in order:
            parts[(d, k)].wait_recv()
            stats[(d, k)].wait_recv()
            pieces.append(
                (
                    part_in[d - 1, k].astype(jnp.float32),
                    column(stat_in[d - 1, k, 0:1, :]),
                    column(stat_in[d - 1, k, 1:2, :]),
                )
            )
        num, top, den = merge(pieces)
        result = (num / den).astype(jnp.bfloat16)
        at_out[k] = result
        for d in range(1, NA):
            at[(d, k)] = send(
                at_out.at[k], at_in.at[d - 1, k], at_s.at[d - 1, k], at_r.at[d - 1, k],
                at_axis("adapter", ada, d, NA),
            )
        wide = result.astype(jnp.float32)
        put_out(att_ref, wide, k)
        own_rank[0] = own_rank[0] + dot_nt(
            from_rows(wide).astype(jnp.bfloat16), od_v[0, :, k * C : (k + 1) * C]
        )

    for k in range(KV):
        remote_parts(k)
        if k == 0:
            l_od.wait()
        if k > 0:
            combine(k - 1)
    combine(KV - 1)

    rk = {}
    ork_out[0] = own_rank[0]
    send_rank(0, ork_out, ork_in, ork_s, ork_r)
    for d in range(1, NA):
        acc = jnp.zeros((N, od_v.shape[1]), jnp.float32)
        for k in range(KV):
            at[(d, k)].wait_recv()
            acc = acc + dot_nt(
                from_rows(at_in[d - 1, k].astype(jnp.float32)).astype(jnp.bfloat16),
                od_v[0, :, k * C : (k + 1) * C],
            )
        ork_out[d] = acc
        send_rank(d, ork_out, ork_in, ork_s, ork_r)

    l_ou.wait()
    ad = {}
    for d in range(1, NA):
        rank = rank_whole(d, ork_out, ork_in)
        for k in range(KV):
            ad_out[d - 1, k] = to_rows(
                dot_nn(rank, ou_v[0, :, k * C : (k + 1) * C])
            ).astype(jnp.bfloat16)
            ad[(d, k)] = send(
                ad_out.at[d - 1, k], ad_in.at[d - 1, k], ad_s.at[d - 1, k],
                ad_r.at[d - 1, k], at_axis("adapter", ada, NA - d, NA),
            )
    rank = rank_whole(0, ork_out, ork_in)
    for k in range(KV):
        own = to_rows(dot_nn(rank, ou_v[0, :, k * C : (k + 1) * C]))
        for d in range(1, NA):
            ad[(d, k)].wait_recv()
        put_out(ada_ref, pick(own, ad_in, k), k)

    for copy in sends:
        copy.wait_send()


def on_device(
    hidden,
    base_query_rows,
    fresh_key_value,
    suffix_key_value,
    suffix_length,
    row_adapter_index,
    prompt_key_value,
    query_down_factors,
    query_up_factors,
    output_down_factors,
    output_up_factors,
):
    NS, NA, NH = lax.axis_size("seq"), lax.axis_size("adapter"), lax.axis_size("head")
    R, T, width = hidden.shape
    D = HEAD_SIZE
    KV = prompt_key_value.shape[2] // D
    G = width // D // KV
    S = suffix_key_value.shape[2]
    N, NG = R * T, R * T * G
    rank = query_down_factors.shape[1]
    assert query_down_factors.shape[0] == 1
    prompt_total = prompt_key_value.shape[1] * NS
    positions = prompt_total + np.arange(S + T, dtype=np.float64)
    frequency = ROPE_BASE ** (-2.0 * np.arange(D // 2, dtype=np.float64) / D)
    angle = positions[:, None] * frequency[None, :]
    cos = np.concatenate([np.cos(angle), np.cos(angle)], 1).astype(np.float32)
    sin = np.concatenate([-np.sin(angle), np.sin(angle)], 1).astype(np.float32)
    bf16, f32 = jnp.bfloat16, jnp.float32
    dma = pltpu.SemaphoreType.DMA
    one = max(NA - 1, 1)
    far = max(NS - 1, 1)
    two = max(NH - 1, 1)

    def like(x):
        return pltpu.VMEM(x.shape, x.dtype)

    scratch = [
        like(hidden),
        like(base_query_rows),
        like(fresh_key_value),
        like(suffix_key_value),
        like(prompt_key_value),
        like(query_down_factors),
        like(query_up_factors),
        like(output_down_factors),
        like(output_up_factors),
        dma((9,)),
        pltpu.VMEM((one,) + hidden.shape, bf16),
        pltpu.VMEM((N, width), f32),
        pltpu.VMEM((NG, D), f32),
        pltpu.VMEM((2, D, KV * D), bf16),
        pltpu.VMEM((-(-N // 16) * 16, KV * D), f32),
        pltpu.VMEM((NA, N, rank), f32),
        pltpu.VMEM((two, NA, N, rank), f32),
        pltpu.VMEM((NA, N, rank), f32),
        pltpu.VMEM((two, NA, N, rank), f32),
        pltpu.VMEM((one, KV, NG, D), bf16),
        pltpu.VMEM((one, KV, NG, D), bf16),
        pltpu.VMEM((KV, NG, D), bf16),
        pltpu.VMEM((far, KV, NG, D), bf16),
        pltpu.VMEM((far, KV, NG, D), bf16),
        pltpu.VMEM((far, KV, NG, D), bf16),
        pltpu.VMEM((far, KV, 2, D), f32),
        pltpu.VMEM((far, KV, 2, D), f32),
        pltpu.VMEM((KV, NG, D), f32),
        pltpu.VMEM((KV, NG, D), f32),
        pltpu.VMEM((KV, NG, D), f32),
        pltpu.VMEM((KV, NG, D), bf16),
        pltpu.VMEM((one, KV, NG, D), bf16),
        pltpu.VMEM((one, KV, NG, D), bf16),
        pltpu.VMEM((one, KV, NG, D), bf16),
        dma((one,)), dma((one,)),
        dma((two, NA)), dma((two, NA)),
        dma((two, NA)), dma((two, NA)),
        dma((one, KV)), dma((one, KV)),
        dma((far, KV)), dma((far, KV)),
        dma((far, KV)), dma((far, KV)),
        dma((far, KV)), dma((far, KV)),
        dma((one, KV)), dma((one, KV)),
        dma((one, KV)), dma((one, KV)),
    ]
    smem = pl.BlockSpec(memory_space=pltpu.SMEM)
    vmem = pl.BlockSpec(memory_space=pltpu.VMEM)
    anywhere = pl.BlockSpec(memory_space=pl.ANY)
    return pl.pallas_call(
        functools.partial(body, (NS, NA, NH, R, T, KV, G, S)),
        out_shape=(
            jax.ShapeDtypeStruct(hidden.shape, bf16),
            jax.ShapeDtypeStruct(hidden.shape, bf16),
        ),
        in_specs=[smem, smem, vmem, vmem] + [anywhere] * 9,
        out_specs=(vmem, vmem),
        scratch_shapes=scratch,
        compiler_params=pltpu.CompilerParams(collective_id=0, has_side_effects=True),
        name="decode",
    )(
        suffix_length,
        row_adapter_index,
        jnp.asarray(cos),
        jnp.asarray(sin),
        hidden,
        base_query_rows,
        fresh_key_value,
        suffix_key_value,
        prompt_key_value,
        query_down_factors,
        query_up_factors,
        output_down_factors,
        output_up_factors,
    )


def solution(mesh):
    rows = P(("groups", "seq", "adapter"), None, "head")
    caches = P(None, ("groups", "seq", "adapter"), None, "head")
    factors = P(("groups", "adapter"), None, "head")
    placed = (
        rows,
        rows,
        caches,
        caches,
        P(("groups", "seq", "adapter")),
        P(("groups", "seq", "adapter"), None),
        P(None, ("groups", "seq"), "head"),
        factors,
        factors,
        factors,
        factors,
    )
    return jax.shard_map(
        on_device, mesh=mesh, in_specs=placed, out_specs=(rows, rows), check_vma=False
    )
```

```python
import functools
import math

import jax
import jax.numpy as jnp
import numpy as np
from jax import lax
from jax.experimental import pallas as pl
from jax.experimental.pallas import tpu as pltpu
from jax.sharding import PartitionSpec as P

HEAD_SIZE = 128
ROPE_BASE = 1000000.0
MESH = pl.DeviceIdType.MESH
NT = (((1,), (1,)), ((), ()))


def dot_nt(a, b):
    return lax.dot_general(a, b, NT, preferred_element_type=jnp.float32)


def dot_nn(a, b):
    return jnp.dot(a, b, preferred_element_type=jnp.float32)


def body(
    cfg,
    len_ref,
    id_ref,
    cos_ref,
    sin_ref,
    hidden_hbm,
    base_hbm,
    fresh_hbm,
    suffix_hbm,
    prompt_hbm,
    qd_hbm,
    qu_hbm,
    od_hbm,
    ou_hbm,
    att_ref,
    ada_ref,
    hidden_v,
    base_v,
    fresh_v,
    suffix_v,
    prompt_v,
    qd_v,
    qu_v,
    od_v,
    ou_v,
    local_sem,
    hid_in,
    tok_f32,
    rows_f32,
    fresh_pad,
    fresh_f32,
    rk_out,
    rk_in,
    ork_out,
    ork_in,
    dl_out,
    dl_in,
    q_own,
    q_in,
    part_out,
    part_in,
    stat_out,
    stat_in,
    own_o,
    own_m,
    own_t,
    at_out,
    at_in,
    ad_out,
    ad_in,
    hid_s,
    hid_r,
    rk_s,
    rk_r,
    ork_s,
    ork_r,
    dl_s,
    dl_r,
    q_s,
    q_r,
    part_s,
    part_r,
    stat_s,
    stat_r,
    at_s,
    at_r,
    ad_s,
    ad_r,
):
    NS, NA, NH, R, T, KV, G, S = cfg
    D = HEAD_SIZE
    N = R * T
    NG = N * G
    C = G * D
    seq, ada, head = lax.axis_index("seq"), lax.axis_index("adapter"), lax.axis_index("head")
    scale = math.log2(math.e) / math.sqrt(D)

    def at_axis(axis, me, offset, size):
        return {axis: lax.rem(me + offset, size)}

    partners = (
        [at_axis("adapter", ada, d, NA) for d in range(1, NA)]
        + [at_axis("head", head, d, NH) for d in range(1, NH)]
        + [at_axis("seq", seq, d, NS) for d in range(1, NS)]
    )
    barrier = pltpu.get_barrier_semaphore()
    for partner in partners:
        pl.semaphore_signal(barrier, inc=1, device_id=partner, device_id_type=MESH)

    loads = []
    for i, (src, dst) in enumerate(
        (
            (hidden_hbm, hidden_v),
            (qd_hbm, qd_v),
            (qu_hbm, qu_v),
            (base_hbm, base_v),
            (prompt_hbm, prompt_v),
            (suffix_hbm, suffix_v),
            (fresh_hbm, fresh_v),
            (od_hbm, od_v),
            (ou_hbm, ou_v),
        )
    ):
        load = pltpu.make_async_copy(src, dst, local_sem.at[i])
        load.start()
        loads.append(load)
    l_hid, l_qd, l_qu, l_base, l_prompt, l_suffix, l_fresh, l_od, l_ou = loads

    pl.semaphore_wait(barrier, len(partners))

    sends = []

    def send(src, dst, s_sem, r_sem, device):
        copy = pltpu.make_async_remote_copy(
            src_ref=src,
            dst_ref=dst,
            send_sem=s_sem,
            recv_sem=r_sem,
            device_id=device,
            device_id_type=MESH,
        )
        copy.start()
        sends.append(copy)
        return copy

    hid = {}
    for d in range(1, NA):
        hid[d] = send(
            hidden_hbm, hid_in.at[d - 1], hid_s.at[d - 1], hid_r.at[d - 1],
            at_axis("adapter", ada, d, NA),
        )

    def gather_tokens(ref):
        for t in range(T):
            tok_f32[t * R : (t + 1) * R, :] = ref[t].astype(jnp.float32)
        return tok_f32[...].astype(jnp.bfloat16)

    rk = {}

    def rank_part(tokens, factors, slot, out_ref, in_ref, s_sem, r_sem):
        out_ref[slot] = dot_nt(tokens, factors)
        send_rank(slot, out_ref, in_ref, s_sem, r_sem)

    def send_rank(slot, out_ref, in_ref, s_sem, r_sem):
        for j in range(1, NH):
            rk[(slot, j)] = send(
                out_ref.at[slot], in_ref.at[j - 1, slot], s_sem.at[j - 1, slot],
                r_sem.at[j - 1, slot], at_axis("head", head, j, NH),
            )

    def rank_whole(slot, out_ref, in_ref):
        total = out_ref[slot]
        for j in range(1, NH):
            rk[(slot, j)].wait_recv()
            total = total + in_ref[j - 1, slot]
        return total.astype(jnp.bfloat16)

    l_hid.wait()
    l_qd.wait()
    rank_part(gather_tokens(hidden_v), qd_v[0], 0, rk_out, rk_in, rk_s, rk_r)
    for d in range(1, NA):
        hid[d].wait_recv()
        rank_part(gather_tokens(hid_in.at[d - 1]), qd_v[0], d, rk_out, rk_in, rk_s, rk_r)

    def to_rows(x):
        for g in range(G):
            rows_f32[pl.ds(g, N, stride=G), :] = x[:, g * D : (g + 1) * D]
        return rows_f32[...]

    def from_rows(x):
        rows_f32[...] = x
        return jnp.concatenate([rows_f32[pl.ds(g, N, stride=G), :] for g in range(G)], 1)

    def put_out(ref, x, k):
        rows_f32[...] = x
        for t in range(T):
            ref[t, :, k * C : (k + 1) * C] = jnp.concatenate(
                [rows_f32[pl.ds(t * R * G + g, R, stride=G), :] for g in range(G)], 1
            ).astype(jnp.bfloat16)

    l_fresh.wait()
    fresh_pad[...] = jnp.zeros_like(fresh_pad)
    for i in range(2):
        fresh_f32[...] = jnp.zeros_like(fresh_f32)
        for t in range(T):
            fresh_f32[t * R : (t + 1) * R, :] = fresh_v[i, t].astype(jnp.float32)
        fresh_pad[i, 0 : fresh_f32.shape[0], :] = fresh_f32[...].astype(jnp.bfloat16)

    l_qu.wait()
    dl = {}
    for d in range(1, NA):
        rank = rank_whole(d, rk_out, rk_in)
        for k in range(KV):
            dl_out[d - 1, k] = to_rows(
                dot_nn(rank, qu_v[0, :, k * C : (k + 1) * C])
            ).astype(jnp.bfloat16)
            dl[(d, k)] = send(
                dl_out.at[d - 1, k], dl_in.at[d - 1, k], dl_s.at[d - 1, k],
                dl_r.at[d - 1, k], at_axis("adapter", ada, NA - d, NA),
            )
    row_of = lax.broadcasted_iota(jnp.int32, (NG, D), 0)
    lane = lax.broadcasted_iota(jnp.int32, (NG, D), 1)
    eye = row_of == lane
    step_of = row_of // (R * G)
    row_index = row_of // G - step_of * R
    ids = jnp.zeros((NG, D), jnp.int32)
    lengths = jnp.zeros((NG, D), jnp.int32)
    for r in range(R):
        ids = jnp.where(row_index == r, id_ref[0, r], ids)
        lengths = jnp.where(row_index == r, len_ref[r], lengths)

    def pick(own, ref, k):
        out = own
        for d in range(1, NA):
            out = jnp.where(
                ids == lax.rem(ada + d, NA), ref[d - 1, k].astype(jnp.float32), out
            )
        return out

    cos = jnp.concatenate(
        [jnp.broadcast_to(cos_ref[pl.ds(len_ref[n % R] + n // R, 1), :], (G, D)) for n in range(N)], 0
    )
    sin = jnp.concatenate(
        [jnp.broadcast_to(sin_ref[pl.ds(len_ref[n % R] + n // R, 1), :], (G, D)) for n in range(N)], 0
    )

    rank = rank_whole(0, rk_out, rk_in)
    l_base.wait()
    qs = {}
    order = sorted(range(1, NS), key=lambda d: (min(d, NS - d), d))
    for k in range(KV):
        delta = to_rows(dot_nn(rank, qu_v[0, :, k * C : (k + 1) * C]))
        for t in range(T):
            x = base_v[t, :, k * C : (k + 1) * C].astype(jnp.float32)
            for g in range(G):
                rows_f32[pl.ds(t * R * G + g, R, stride=G), :] = x[:, g * D : (g + 1) * D]
        base = rows_f32[...]
        for d in range(1, NA):
            dl[(d, k)].wait_recv()
        merged = base + pick(delta, dl_in, k)
        turned = merged * cos + pltpu.roll(merged, D // 2, 1) * sin
        q_own[k] = turned.astype(jnp.bfloat16)
        for d in order:
            qs[(d, k)] = send(
                q_own.at[k], q_in.at[d - 1, k], q_s.at[d - 1, k], q_r.at[d - 1, k],
                at_axis("seq", seq, d, NS),
            )

    l_prompt.wait()
    l_suffix.wait()

    def values_of(v):
        return jnp.concatenate([v, jnp.ones((v.shape[0], D), jnp.bfloat16)], 1)

    def prompt_part(query, k):
        cols = slice(k * D, (k + 1) * D)
        scores = dot_nt(query, prompt_v[0, :, cols])
        peak = jnp.max(scores, -1, keepdims=True)
        weight = jnp.exp2((scores - peak) * scale).astype(jnp.bfloat16)
        both = dot_nn(weight, values_of(prompt_v[1, :, cols]))
        return both[:, :D], peak, both[:, D:]

    def local_part(query, k):
        cols = slice(k * D, (k + 1) * D)
        n_suf = R * S
        s_keys = suffix_v[0, :, :, cols].reshape(n_suf, D)
        s_vals = suffix_v[1, :, :, cols].reshape(n_suf, D)
        scores = jnp.concatenate(
            [dot_nt(query, s_keys), dot_nt(query, fresh_pad[0, :, cols])], 1
        )
        masked = jnp.where(admitted, scores, -1e30)
        peak = jnp.max(masked, -1, keepdims=True)
        weight = jnp.where(admitted, jnp.exp2((masked - peak) * scale), 0.0).astype(jnp.bfloat16)
        both = dot_nn(
            weight, values_of(jnp.concatenate([s_vals, fresh_pad[1, :, cols]], 0))
        )
        return both[:, :D], peak, both[:, D:]

    n_suf = R * S
    s_row = lax.broadcasted_iota(jnp.int32, (NG, n_suf), 0) // G % R
    s_col = lax.broadcasted_iota(jnp.int32, (NG, n_suf), 1)
    s_len = jnp.concatenate([lengths] * (n_suf // D), 1)
    in_suffix = (s_col // S == s_row) & (s_col - s_row * S < s_len)
    in_fresh = (lane % R == row_index) & (lane // R <= step_of)
    admitted = jnp.concatenate(
        [in_suffix.astype(jnp.int32), in_fresh.astype(jnp.int32)], 1
    ) != 0

    def merge(parts):
        top = functools.reduce(jnp.maximum, [p[1] for p in parts])
        factors = [jnp.exp2((p[1] - top) * scale) for p in parts]
        num = functools.reduce(jnp.add, [p[0] * f for p, f in zip(parts, factors)])
        den = functools.reduce(jnp.add, [p[2] * f for p, f in zip(parts, factors)])
        return num, top, den

    for k in range(KV):
        query = q_own[k]
        o, m, t = merge([prompt_part(query, k), local_part(query, k)])
        own_o[k] = o
        own_m[k] = jnp.broadcast_to(m, (NG, D))
        own_t[k] = t

    parts, stats = {}, {}

    def remote_parts(k):
        for d in order:
            qs[(d, k)].wait_recv()
            o, m, t = prompt_part(q_in[d - 1, k], k)
            part_out[d - 1, k] = o.astype(jnp.bfloat16)
            stat_out[d - 1, k, 0:1, 0:D] = jnp.sum(jnp.where(eye, m, 0.0), 0, keepdims=True)
            stat_out[d - 1, k, 1:2, 0:D] = jnp.sum(jnp.where(eye, t, 0.0), 0, keepdims=True)
            home = at_axis("seq", seq, NS - d, NS)
            parts[(d, k)] = send(
                part_out.at[d - 1, k], part_in.at[d - 1, k], part_s.at[d - 1, k],
                part_r.at[d - 1, k], home,
            )
            stats[(d, k)] = send(
                stat_out.at[d - 1, k], stat_in.at[d - 1, k], stat_s.at[d - 1, k],
                stat_r.at[d - 1, k], home,
            )

    at = {}
    own_rank = [jnp.zeros((N, od_v.shape[1]), jnp.float32)]

    def column(row):
        return jnp.sum(jnp.where(eye, row, 0.0), 1, keepdims=True)

    def combine(k):
        pieces = [(own_o[k], own_m[k], own_t[k])]
        for d in order:
            parts[(d, k)].wait_recv()
            stats[(d, k)].wait_recv()
            pieces.append(
                (
                    part_in[d - 1, k].astype(jnp.float32),
                    column(stat_in[d - 1, k, 0:1, :]),
                    column(stat_in[d - 1, k, 1:2, :]),
                )
            )
        num, top, den = merge(pieces)
        result = (num / den).astype(jnp.bfloat16)
        at_out[k] = result
        for d in range(1, NA):
            at[(d, k)] = send(
                at_out.at[k], at_in.at[d - 1, k], at_s.at[d - 1, k], at_r.at[d - 1, k],
                at_axis("adapter", ada, d, NA),
            )
        wide = result.astype(jnp.float32)
        put_out(att_ref, wide, k)
        own_rank[0] = own_rank[0] + dot_nt(
            from_rows(wide).astype(jnp.bfloat16), od_v[0, :, k * C : (k + 1) * C]
        )

    for k in range(KV):
        remote_parts(k)
        if k == 0:
            l_od.wait()
        if k > 0:
            combine(k - 1)
    combine(KV - 1)

    rk = {}
    ork_out[0] = own_rank[0]
    send_rank(0, ork_out, ork_in, ork_s, ork_r)
    for d in range(1, NA):
        acc = jnp.zeros((N, od_v.shape[1]), jnp.float32)
        for k in range(KV):
            at[(d, k)].wait_recv()
            acc = acc + dot_nt(
                from_rows(at_in[d - 1, k].astype(jnp.float32)).astype(jnp.bfloat16),
                od_v[0, :, k * C : (k + 1) * C],
            )
        ork_out[d] = acc
        send_rank(d, ork_out, ork_in, ork_s, ork_r)

    l_ou.wait()
    ad = {}
    for d in range(1, NA):
        rank = rank_whole(d, ork_out, ork_in)
        for k in range(KV):
            ad_out[d - 1, k] = to_rows(
                dot_nn(rank, ou_v[0, :, k * C : (k + 1) * C])
            ).astype(jnp.bfloat16)
            ad[(d, k)] = send(
                ad_out.at[d - 1, k], ad_in.at[d - 1, k], ad_s.at[d - 1, k],
                ad_r.at[d - 1, k], at_axis("adapter", ada, NA - d, NA),
            )
    rank = rank_whole(0, ork_out, ork_in)
    for k in range(KV):
        own = to_rows(dot_nn(rank, ou_v[0, :, k * C : (k + 1) * C]))
        for d in range(1, NA):
            ad[(d, k)].wait_recv()
        put_out(ada_ref, pick(own, ad_in, k), k)

    for copy in sends:
        copy.wait_send()


def finish(first, second, att_ref, ada_ref):
    att_ref[...] = first[...]
    ada_ref[...] = second[...]


def on_device(
    hidden,
    base_query_rows,
    fresh_key_value,
    suffix_key_value,
    suffix_length,
    row_adapter_index,
    prompt_key_value,
    query_down_factors,
    query_up_factors,
    output_down_factors,
    output_up_factors,
):
    NS, NA, NH = lax.axis_size("seq"), lax.axis_size("adapter"), lax.axis_size("head")
    hidden, base_query_rows = (x.transpose(1, 0, 2) for x in (hidden, base_query_rows))
    fresh_key_value = fresh_key_value.transpose(0, 2, 1, 3)
    T, R, width = hidden.shape
    D = HEAD_SIZE
    KV = prompt_key_value.shape[2] // D
    G = width // D // KV
    S = suffix_key_value.shape[2]
    N, NG = R * T, R * T * G
    rank = query_down_factors.shape[1]
    assert query_down_factors.shape[0] == 1
    prompt_total = prompt_key_value.shape[1] * NS
    positions = prompt_total + np.arange(S + T, dtype=np.float64)
    frequency = ROPE_BASE ** (-2.0 * np.arange(D // 2, dtype=np.float64) / D)
    angle = positions[:, None] * frequency[None, :]
    cos = np.concatenate([np.cos(angle), np.cos(angle)], 1).astype(np.float32)
    sin = np.concatenate([-np.sin(angle), np.sin(angle)], 1).astype(np.float32)
    bf16, f32 = jnp.bfloat16, jnp.float32
    dma = pltpu.SemaphoreType.DMA
    one = max(NA - 1, 1)
    far = max(NS - 1, 1)
    two = max(NH - 1, 1)

    def like(x):
        return pltpu.VMEM(x.shape, x.dtype)

    scratch = [
        like(hidden),
        like(base_query_rows),
        like(fresh_key_value),
        like(suffix_key_value),
        like(prompt_key_value),
        like(query_down_factors),
        like(query_up_factors),
        like(output_down_factors),
        like(output_up_factors),
        dma((9,)),
        pltpu.VMEM((one,) + hidden.shape, bf16),
        pltpu.VMEM((N, width), f32),
        pltpu.VMEM((NG, D), f32),
        pltpu.VMEM((2, D, KV * D), bf16),
        pltpu.VMEM((-(-N // 16) * 16, KV * D), f32),
        pltpu.VMEM((NA, N, rank), f32),
        pltpu.VMEM((two, NA, N, rank), f32),
        pltpu.VMEM((NA, N, rank), f32),
        pltpu.VMEM((two, NA, N, rank), f32),
        pltpu.VMEM((one, KV, NG, D), bf16),
        pltpu.VMEM((one, KV, NG, D), bf16),
        pltpu.VMEM((KV, NG, D), bf16),
        pltpu.VMEM((far, KV, NG, D), bf16),
        pltpu.VMEM((far, KV, NG, D), bf16),
        pltpu.VMEM((far, KV, NG, D), bf16),
        pltpu.VMEM((far, KV, 2, D), f32),
        pltpu.VMEM((far, KV, 2, D), f32),
        pltpu.VMEM((KV, NG, D), f32),
        pltpu.VMEM((KV, NG, D), f32),
        pltpu.VMEM((KV, NG, D), f32),
        pltpu.VMEM((KV, NG, D), bf16),
        pltpu.VMEM((one, KV, NG, D), bf16),
        pltpu.VMEM((one, KV, NG, D), bf16),
        pltpu.VMEM((one, KV, NG, D), bf16),
        dma((one,)), dma((one,)),
        dma((two, NA)), dma((two, NA)),
        dma((two, NA)), dma((two, NA)),
        dma((one, KV)), dma((one, KV)),
        dma((far, KV)), dma((far, KV)),
        dma((far, KV)), dma((far, KV)),
        dma((far, KV)), dma((far, KV)),
        dma((one, KV)), dma((one, KV)),
        dma((one, KV)), dma((one, KV)),
    ]
    smem = pl.BlockSpec(memory_space=pltpu.SMEM)
    vmem = pl.BlockSpec(memory_space=pltpu.VMEM)
    anywhere = pl.BlockSpec(memory_space=pl.ANY)
    results = pl.pallas_call(
        functools.partial(body, (NS, NA, NH, R, T, KV, G, S)),
        out_shape=(
            jax.ShapeDtypeStruct(hidden.shape, bf16),
            jax.ShapeDtypeStruct(hidden.shape, bf16),
        ),
        in_specs=[smem, smem, vmem, vmem] + [anywhere] * 9,
        out_specs=(vmem, vmem),
        scratch_shapes=scratch,
        compiler_params=pltpu.CompilerParams(collective_id=0, has_side_effects=True),
        name="decode",
    )(
        suffix_length,
        row_adapter_index.transpose(1, 0),
        jnp.asarray(cos),
        jnp.asarray(sin),
        hidden,
        base_query_rows,
        fresh_key_value,
        suffix_key_value,
        prompt_key_value,
        query_down_factors,
        query_up_factors,
        output_down_factors,
        output_up_factors,
    )
    results = pl.pallas_call(
        finish,
        out_shape=tuple(jax.ShapeDtypeStruct(x.shape, bf16) for x in results),
        in_specs=[vmem, vmem],
        out_specs=(vmem, vmem),
        name="finish",
    )(*results)
    return tuple(x.transpose(1, 0, 2) for x in results)


def solution(mesh):
    rows = P(("groups", "seq", "adapter"), None, "head")
    caches = P(None, ("groups", "seq", "adapter"), None, "head")
    factors = P(("groups", "adapter"), None, "head")
    placed = (
        rows,
        rows,
        caches,
        caches,
        P(("groups", "seq", "adapter")),
        P(("groups", "seq", "adapter"), None),
        P(None, ("groups", "seq"), "head"),
        factors,
        factors,
        factors,
        factors,
    )
    return jax.shard_map(
        on_device, mesh=mesh, in_specs=placed, out_specs=(rows, rows), check_vma=False
    )
```
